32 devices in a mesh: groups: 2 (over y), row: 4 (over x, core), col: 4 (over z).
Axes of the slice: x: 2, y: 2, z: 4, core: 2. Of those that a mesh axis runs over, the one named last changes fastest.
Arguments:
- hidden_in: bfloat16 [1024, 6144], P(('groups', 'col'), 'row'), parts along dimension 0, may hold values from -6 to 6
- gate_proj: bfloat16 [6144, 14336], P('row', 'col'), may hold values from -0.078125 to 0.078125
- up_proj: bfloat16 [6144, 14336], P('row', 'col'), may hold values from -0.078125 to 0.078125
- down_proj: bfloat16 [14336, 6144], P('col', 'row'), may hold values from -0.046875 to 0.046875
- out_grad: bfloat16 [1024, 6144], P(('groups', 'col'), 'row'), parts along dimension 0, may hold values from -1.0546875 to 1.0546875
Outputs:
- layer_out: bfloat16 [1024, 6144], P(('groups', 'col'), 'row'), parts along dimension 0
- in_grad: bfloat16 [1024, 6144], P(('groups', 'col'), 'row'), parts along dimension 0
- gate_grad: bfloat16 [12288, 14336], P(('groups', 'row'), 'col'), parts along dimension 0
- up_grad: bfloat16 [12288, 14336], P(('groups', 'row'), 'col'), parts along dimension 0
- down_grad: bfloat16 [28672, 6144], P(('groups', 'col'), 'row'), parts along dimension 0
The draws below stay inside these ranges and needn't reach their ends.
There are 2 independent parts, one for each index of `groups`. The reference program is written for one: setup_inputs(seed, part) draws one part's arguments, and reference() takes and returns one part's arrays. A program takes and returns all parts, laid end to end along the dimension named above; an argument that names none is the same for every part. Nothing has to cross between parts.
All inputs are finite; a program needn't handle non-finite values.
Results may differ from the reference program's by a relative error of at most 0.02.
Values may be sent and summed in bfloat16 or wider, within the bound.
No kernel may reach another device: no remote copies, remote signals or barrier semaphores. Data moves between devices by JAX's collectives and lax.ppermute only.
A program may use at most 192 MiB of HBM per device.

```python
import jax
import jax.numpy as jnp

D = 6144
FF = 14336
TOKENS = 512
N_ROW = 4
N_COL = 4


def level_of(key, shape, split, least, high):
    loudness = 1.0
    for axis_at, shards_of in split:
        draws = jax.random.uniform(jax.random.fold_in(jax.random.fold_in(key, 6), axis_at), (shards_of,), jnp.float32, least / len(split), high / len(split))
        loudness = loudness * jnp.repeat(jnp.exp(draws), shape[axis_at] // shards_of).reshape((-1,) + (1,) * (len(shape) - 1 - axis_at))
    return loudness


def normal_values(key, shape, spread, limit, shards=(), dtype=jnp.bfloat16):
    drawn = spread * jax.random.normal(key, shape, jnp.float32)
    if shards:
        drawn = drawn * level_of(key, shape, shards, -0.22, 0.18)
    return jnp.clip(drawn, -limit, limit).astype(dtype)


def setup_inputs(seed: int = 0, part: int = 0) -> dict:
    streams_of = jax.random.split(jax.random.key(seed), 6)
    part_splits = jax.random.split(jax.random.fold_in(streams_of[5], part), 6)
    hidden_in = normal_values(part_splits[0], (TOKENS, D), 1.0, 6.0, ((0, 4), (1, 4)))
    gate_proj = normal_values(streams_of[1], (D, FF), D ** -0.5, 0.078125, ((0, 4), (1, 4)))
    up_proj = normal_values(streams_of[2], (D, FF), D ** -0.5, 0.078125, ((0, 4), (1, 4)))
    down_proj = normal_values(streams_of[3], (FF, D), FF ** -0.5, 0.046875, ((0, 4), (1, 4)))
    out_grad = normal_values(part_splits[4], (TOKENS, D), (4.0 / TOKENS ** 0.5), 1.0546875, ((0, 4), (1, 4)))
    return {"hidden_in": hidden_in, "gate_proj": gate_proj, "up_proj": up_proj, "down_proj": down_proj, "out_grad": out_grad}


def block_sum(pairs, blocks):
    inner = pairs[0][0].shape[1]
    width = inner // blocks
    total = None
    for index in range(blocks):
        partial_value = None
        for left, right in pairs:
            term = jnp.dot(left[:, index * width:(index + 1) * width], right[index * width:(index + 1) * width, :], preferred_element_type=jnp.float32)
            partial_value = term if partial_value is None else partial_value + term
        rounded = partial_value.astype(jnp.bfloat16).astype(jnp.float32)
        total = rounded if total is None else total + rounded
    return total


def reference(hidden_in, gate_proj, up_proj, down_proj, out_grad):
    gate_act = block_sum([(hidden_in, gate_proj)], N_ROW)
    up_act = block_sum([(hidden_in, up_proj)], N_ROW)
    logistic = jax.nn.sigmoid(gate_act)
    swish_act = gate_act * logistic
    hidden = (swish_act * up_act).astype(jnp.bfloat16)
    layer_out = block_sum([(hidden, down_proj)], N_COL).astype(jnp.bfloat16)
    hid_grad = block_sum([(out_grad, down_proj.T)], N_ROW)
    gate_delta = (hid_grad * up_act * logistic * (1.0 + gate_act * (1.0 - logistic))).astype(jnp.bfloat16)
    up_delta = (hid_grad * swish_act).astype(jnp.bfloat16)
    down_grad = jnp.dot(hidden.T, out_grad, preferred_element_type=jnp.float32).astype(jnp.bfloat16)
    gate_grad = jnp.dot(hidden_in.T, gate_delta, preferred_element_type=jnp.float32).astype(jnp.bfloat16)
    up_grad = jnp.dot(hidden_in.T, up_delta, preferred_element_type=jnp.float32).astype(jnp.bfloat16)
    in_grad = block_sum([(gate_delta, gate_proj.T), (up_delta, up_proj.T)], N_COL).astype(jnp.bfloat16)
    return (layer_out, in_grad, gate_grad, up_grad, down_grad)
```

```python
import functools

import jax
import jax.numpy as jnp
from jax import lax
from jax.experimental import pallas as pl
from jax.experimental.pallas import tpu as pltpu
from jax.sharding import PartitionSpec as P

F32 = jnp.float32
BF16 = jnp.bfloat16
VMEM_LIMIT = 56 * 2**20


def swiglu_parts(gate_act, up_act):
    logistic = jax.nn.sigmoid(gate_act)
    swish_act = gate_act * logistic
    hidden = (swish_act * up_act).astype(BF16)
    return (logistic, swish_act, hidden)


def make_deltas(hid_grad, gate_act, up_act, logistic, swish_act):
    gate_delta = (hid_grad * up_act * logistic * (1.0 + gate_act * (1.0 - logistic))).astype(BF16)
    up_delta = (hid_grad * swish_act).astype(BF16)
    return (gate_delta, up_delta)


def last_product(left, right):
    return lax.dot_general(left, right, (((1,), (1,)), ((), ())), preferred_element_type=F32)


def first_product(left, right):
    return lax.dot_general(left, right, (((0,), (0,)), ((), ())), preferred_element_type=F32)


def plain_product(left, right):
    return lax.dot_general(left, right, (((1,), (0,)), ((), ())), preferred_element_type=F32)


def general_body(hidden_in, gate_proj, up_proj, down_proj, out_grad):
    inputs_all = lax.all_gather(hidden_in, "col", axis=0, tiled=True)
    gate_act, up_act = (
        lax.psum_scatter(
            plain_product(inputs_all, proj).astype(BF16), "row", scatter_dimension=0, tiled=True
        ).astype(F32)
        for proj in (gate_proj, up_proj)
    )
    logistic, swish_act, hidden = swiglu_parts(gate_act, up_act)
    hidden_all = lax.all_gather(hidden, "row", axis=0, tiled=True)
    layer_out = lax.psum_scatter(
        plain_product(hidden_all, down_proj).astype(BF16), "col", scatter_dimension=0, tiled=True
    )
    grads_all = lax.all_gather(out_grad, "col", axis=0, tiled=True)
    hid_grad = lax.psum_scatter(
        last_product(grads_all, down_proj).astype(BF16), "row", scatter_dimension=0, tiled=True
    ).astype(F32)
    gate_delta, up_delta = make_deltas(hid_grad, gate_act, up_act, logistic, swish_act)
    gate_full = lax.all_gather(gate_delta, "row", axis=0, tiled=True)
    up_full = lax.all_gather(up_delta, "row", axis=0, tiled=True)
    down_grad = first_product(hidden_all, grads_all).astype(BF16)
    gate_grad = first_product(inputs_all, gate_full).astype(BF16)
    up_grad = first_product(inputs_all, up_full).astype(BF16)
    in_grad = lax.psum_scatter(
        (last_product(gate_full, gate_proj) + last_product(up_full, up_proj)).astype(BF16),
        "col",
        scatter_dimension=0,
        tiled=True,
    )
    return (layer_out, in_grad, gate_grad, up_grad, down_grad)


def call(kernel, core, operands, in_specs, out_specs, out_shape, grid, scratch, flops, moved):
    return pl.pallas_call(
        kernel,
        grid_spec=pltpu.PrefetchScalarGridSpec(
            num_scalar_prefetch=1,
            grid=grid,
            in_specs=in_specs,
            out_specs=out_specs,
            scratch_shapes=scratch,
        ),
        out_shape=out_shape,
        compiler_params=pltpu.CompilerParams(vmem_limit_bytes=VMEM_LIMIT),
        cost_estimate=pl.CostEstimate(flops=1, bytes_accessed=1, transcendentals=0),
    )(core, *operands)


def whole(array):
    return pl.BlockSpec(array.shape, lambda i, core: (0,) * array.ndim, pipeline_mode=pl.Buffered(1))


def rows_of(refs, store):
    at = 0
    for ref in refs:
        store[at : at + ref.shape[0], :] = ref[...]
        at += ref.shape[0]


def project(half, inputs, weights, transposed, tile, groups, added=None):
    tokens = sum(array.shape[0] for array in inputs)
    depth = inputs[0].shape[1]
    units = weights[0].shape[0 if transposed else 1] // 2
    steps = units // tile
    count = len(weights)
    starts = [sum(groups[:index]) for index in range(len(groups))]

    def kernel(half_ref, *refs):
        step = pl.program_id(0)
        input_refs, refs = refs[: len(inputs)], refs[len(inputs) :]
        weight_refs, refs = refs[:count], refs[count:]
        if added is not None:
            added_refs, refs = refs[: len(added)], refs[len(added) :]
        out_refs = refs[: len(groups) * (1 if added is not None else count)]
        if len(inputs) > 1:
            left_ref = refs[len(out_refs)]

            @pl.when(step == 0)
            def _():
                rows_of(input_refs, left_ref)
        else:
            left_ref = input_refs[0]
        for index in range(count):

            @pl.when(step // steps == index)
            def _():
                product = last_product if transposed else plain_product
                total = product(left_ref[...], weight_refs[index][...])
                for group, (start, size) in enumerate(zip(starts, groups)):
                    part = total[start : start + size]
                    if added is not None:
                        part = part + added_refs[index * len(groups) + group][...].astype(F32)
                        out_refs[group][0] = part.astype(BF16)
                    else:
                        out_refs[index * len(groups) + group][...] = part.astype(BF16)

    def tile_at(i, index):
        return jnp.clip(i - index * steps, 0, steps - 1)

    def weight_spec(index):
        if transposed:
            return pl.BlockSpec((tile, depth), lambda i, half: (half[0] * steps + tile_at(i, index), 0))
        return pl.BlockSpec((depth, tile), lambda i, half: (0, half[0] * steps + tile_at(i, index)))

    single_specs = [
        pl.BlockSpec((size, tile), lambda i, half, index=index: (0, tile_at(i, index)))
        for index in range(count)
        for size in groups
    ]
    in_specs = [*map(whole, inputs), *map(weight_spec, range(count))]
    if added is None:
        out_specs = single_specs
        out_shape = [jax.ShapeDtypeStruct((size, units), BF16) for _ in range(count) for size in groups]
    else:
        in_specs += single_specs
        out_specs = [pl.BlockSpec((1, size, tile), lambda i, half: (i // steps, 0, i % steps)) for size in groups]
        out_shape = [jax.ShapeDtypeStruct((count, size, units), BF16) for size in groups]
    return call(
        kernel,
        half,
        [*inputs, *weights, *(added or ())],
        in_specs,
        out_specs,
        out_shape,
        (count * steps,),
        [pltpu.VMEM((tokens, depth), BF16)] if len(inputs) > 1 else [],
        2 * tokens * depth * units * count,
        2 * (count * units * (depth + tokens) + tokens * depth),
    )


def sums(near_ref, far_ref, index):
    return near_ref[index].astype(F32) + far_ref[index].astype(F32)


def activate(core, near, far, tile):
    _, tokens, units = near.shape

    def kernel(core_ref, near_ref, far_ref, out_ref):
        gate, up = sums(near_ref, far_ref, 0), sums(near_ref, far_ref, 1)
        out_ref[...] = (gate * jax.nn.sigmoid(gate) * up).astype(BF16)

    pair = pl.BlockSpec((2, tokens, tile), lambda i, core: (0, 0, i))
    return call(
        kernel,
        core,
        [near, far],
        [pair, pair],
        pl.BlockSpec((tokens, tile), lambda i, core: (0, i)),
        jax.ShapeDtypeStruct((tokens, units), BF16),
        (units // tile,),
        [],
        10 * tokens * units,
        10 * tokens * units,
    )


def deltas(core, near, far, near_grad, far_grad, tile):
    _, tokens, units = far_grad.shape

    def kernel(core_ref, near_ref, far_ref, near_grad_ref, far_grad_ref, out_ref):
        gate, up = sums(near_ref, far_ref, 0), sums(near_ref, far_ref, 1)
        grad = sums(near_grad_ref, far_grad_ref, 0)
        logistic = jax.nn.sigmoid(gate)
        out_ref[0] = (grad * up * logistic * (1.0 + gate * (1.0 - logistic))).astype(BF16)
        out_ref[1] = (grad * (gate * logistic)).astype(BF16)

    pair = pl.BlockSpec((2, tokens, tile), lambda i, core: (0, 0, i))
    return call(
        kernel,
        core,
        [near, far, near_grad, far_grad],
        [
            pair,
            pair,
            pl.BlockSpec((1, tokens, tile), lambda i, core: (0, 0, i)),
            pl.BlockSpec((1, tokens, tile), lambda i, core: (0, 0, i)),
        ],
        pl.BlockSpec((2, tokens, tile), lambda i, core: (0, 0, i)),
        jax.ShapeDtypeStruct((2, tokens, units), BF16),
        (units // tile,),
        [],
        10 * tokens * units,
        16 * tokens * units,
    )


def out_parts(core, own, other, down_proj, chunk, tile):
    units, width = own[0].shape[1], down_proj.shape[1]
    tokens = sum(array.shape[0] for array in own)
    chunks = tokens // chunk

    def kernel(core_ref, *refs):
        own_refs, refs = refs[: len(own)], refs[len(own) :]
        other_refs, refs = refs[: len(other)], refs[len(other) :]
        own_down, other_down = refs[:2]
        out_refs = refs[2 : 2 + chunks]
        own_store, other_store = refs[2 + chunks :]

        @pl.when(pl.program_id(0) == 0)
        def _():
            rows_of(own_refs, own_store)
            rows_of(other_refs, other_store)

        total = plain_product(own_store[...], own_down[...])
        total = total + plain_product(other_store[...], other_down[...])
        for index, out_ref in enumerate(out_refs):
            out_ref[...] = total[index * chunk : (index + 1) * chunk].astype(BF16)

    return call(
        kernel,
        core,
        [*own, *other, down_proj, down_proj],
        [
            *map(whole, own),
            *map(whole, other),
            pl.BlockSpec((units, tile), lambda i, core: (core[0], i)),
            pl.BlockSpec((units, tile), lambda i, core: (1 - core[0], i)),
        ],
        [pl.BlockSpec((chunk, tile), lambda i, core: (0, i))] * chunks,
        [jax.ShapeDtypeStruct((chunk, width), BF16)] * chunks,
        (width // tile,),
        [pltpu.VMEM((tokens, units), BF16)] * 2,
        4 * tokens * units * width,
        2 * (2 * units * (width + tokens) + tokens * width),
    )


def in_parts(core, own, other, gate_proj, up_proj, chunk, tile):
    _, tokens, units = own.shape
    width = gate_proj.shape[0]
    chunks = tokens // chunk

    def kernel(core_ref, own_ref, other_ref, own_gate, other_gate, own_up, other_up, *out_refs):
        total = last_product(own_ref[0], own_gate[...]) + last_product(other_ref[0], other_gate[...])
        total = total + last_product(own_ref[1], own_up[...])
        total = total + last_product(other_ref[1], other_up[...])
        for index, out_ref in enumerate(out_refs):
            out_ref[...] = total[index * chunk : (index + 1) * chunk].astype(BF16)

    own_spec = pl.BlockSpec((tile, units), lambda i, core: (i, core[0]))
    other_spec = pl.BlockSpec((tile, units), lambda i, core: (i, 1 - core[0]))
    return call(
        kernel,
        core,
        [own, other, gate_proj, gate_proj, up_proj, up_proj],
        [whole(own), whole(other), own_spec, other_spec, own_spec, other_spec],
        [pl.BlockSpec((chunk, tile), lambda i, core: (0, i))] * chunks,
        [jax.ShapeDtypeStruct((chunk, width), BF16)] * chunks,
        (width // tile,),
        [],
        8 * tokens * units * width,
        2 * (4 * units * (width + tokens) + tokens * width),
    )


def down_weight_grad(core, own, other, grads, tile):
    units, width = own[0].shape[1], grads[0].shape[1]
    tokens = sum(array.shape[0] for array in grads)
    steps = units // tile

    def kernel(core_ref, *refs):
        own_refs, refs = refs[: len(own)], refs[len(own) :]
        other_refs, refs = refs[: len(other)], refs[len(other) :]
        grad_refs, refs = refs[: len(grads)], refs[len(grads) :]
        out_ref, left, right = refs
        step = pl.program_id(0)

        @pl.when(step == 0)
        def _():
            rows_of(own_refs, left.at[0])
            rows_of(other_refs, left.at[1])
            rows_of(grad_refs, right)

        at = pl.multiple_of((step % steps) * tile, 128)
        out_ref[...] = first_product(left[step // steps, :, pl.ds(at, tile)], right[...]).astype(BF16)

    def out_at(i, core):
        return (jnp.where(i < steps, core[0], 1 - core[0]) * steps + i % steps, 0)

    return call(
        kernel,
        core,
        [*own, *other, *grads],
        [*map(whole, own), *map(whole, other), *map(whole, grads)],
        pl.BlockSpec((tile, width), out_at),
        jax.ShapeDtypeStruct((2 * units, width), BF16),
        (2 * steps,),
        [pltpu.VMEM((2, tokens, units), BF16), pltpu.VMEM((tokens, width), BF16)],
        4 * tokens * units * width,
        2 * (2 * units * (width + tokens) + tokens * width),
    )


def weight_grads(core, inputs, own, other, tile):
    depth, units = inputs[0].shape[1], own[0].shape[2]
    tokens = sum(array.shape[0] for array in inputs)
    steps = depth // tile

    def kernel(core_ref, *refs):
        input_refs, refs = refs[: len(inputs)], refs[len(inputs) :]
        own_refs, refs = refs[: len(own)], refs[len(own) :]
        other_refs, refs = refs[: len(other)], refs[len(other) :]
        gate_ref, up_ref, left, right = refs
        step = pl.program_id(0)

        @pl.when(step == 0)
        def _():
            rows_of(input_refs, left)
            for side, side_refs in enumerate((own_refs, other_refs)):
                for index in range(2):
                    rows_of([ref.at[index] for ref in side_refs], right.at[side, index])

        columns = left[:, pl.ds(pl.multiple_of((step % steps) * tile, 128), tile)]
        for index, out_ref in enumerate((gate_ref, up_ref)):

            @pl.when(step // steps == index)
            def _():
                for side in range(2):
                    half = core_ref[0] if side == 0 else 1 - core_ref[0]
                    out_ref[:, pl.ds(pl.multiple_of(half * units, 128), units)] = first_product(
                        columns, right[side, index]
                    ).astype(BF16)

    return call(
        kernel,
        core,
        [*inputs, *own, *other],
        [*map(whole, inputs), *map(whole, own), *map(whole, other)],
        [
            pl.BlockSpec((tile, 2 * units), lambda i, core: (jnp.clip(i, 0, steps - 1), 0)),
            pl.BlockSpec((tile, 2 * units), lambda i, core: (jnp.clip(i - steps, 0, steps - 1), 0)),
        ],
        [jax.ShapeDtypeStruct((depth, 2 * units), BF16)] * 2,
        (2 * steps,),
        [pltpu.VMEM((tokens, depth), BF16), pltpu.VMEM((2, 2, tokens, units), BF16)],
        8 * tokens * units * depth,
        2 * (4 * units * (depth + tokens) + tokens * depth),
    )


def paired_body(cols, hidden_in, gate_proj, up_proj, down_proj, out_grad):
    chunk = hidden_in.shape[0]
    core = (lax.axis_index("row") % 2).astype(jnp.int32).reshape(1)
    other_core = 1 - core
    ring = [(i, (i + 1) % cols) for i in range(cols)]

    def along(array):
        return lax.ppermute(array, "col", ring)

    def to_core(array):
        return lax.ppermute(array, "row", [(0, 1), (1, 0), (2, 3), (3, 2)])

    def to_chip(array):
        return lax.ppermute(array, "row", [(0, 2), (2, 0), (1, 3), (3, 1)])

    last = [None]

    def after(array):
        if last[0] is None:
            return array
        return lax.optimization_barrier((array, last[0]))[0]

    def note(array):
        last[0] = array
        return array

    def add(left, right):
        return note((after(left).astype(F32) + right.astype(F32)).astype(BF16))

    inputs = [hidden_in]
    for _ in range(cols - 1):
        inputs.append(along(inputs[-1]))
    grads = [lax.optimization_barrier((out_grad, inputs[-1]))[0]]
    for _ in range(cols - 1):
        grads.append(along(grads[-1]))

    groups = [(0,), (1,), (2, 3)]
    near, far, own, other = [None] * 3, [None] * 3, [None] * 3, [None] * 3

    def act(group):
        own[group] = note(activate(core, near[group], after(far[group]), 896))
        other[group] = to_core(own[group])

    for index, group in enumerate(groups):
        chunks = [inputs[k] for k in group]
        sizes = [chunk * len(group)]
        first = after(chunks[-1])
        sent = project(other_core, [*chunks[:-1], first], [gate_proj, up_proj], False, 896, sizes)
        note(sent[0])
        (near[index],) = project(
            core, chunks, [gate_proj, up_proj], False, 896, sizes, list(map(to_core, sent))
        )
        note(near[index])
        far[index] = to_chip(near[index])
        if index:
            act(index - 1)

    sizes = [chunk, 2 * chunk, chunk]
    rows = [grads[k] for k in (1, 2, 3, 0)]
    sent = project(other_core, [*rows[:-1], after(rows[-1])], [down_proj], True, 896, sizes)
    note(sent[0])
    sent = project(core, rows, [down_proj], True, 896, sizes, list(map(to_core, sent)))
    note(sent[0])
    near_grads = {1: sent[0], 2: sent[1], 0: sent[2]}
    far_grads = {group: to_chip(part) for group, part in near_grads.items()}
    act(2)

    out_part = out_parts(core, own, [*other[:-1], after(other[-1])], down_proj, chunk, 512)
    note(out_part[0])
    out_sent = along(out_part[1])
    down_grad = note(down_weight_grad(core, own, [*other[:-1], after(other[-1])], grads, 896))

    own_delta, other_delta, in_part = {}, {}, {}
    in_sent = None
    for group in (1, 2, 0):
        far_grad = after(far_grads[group])
        own_delta[group] = note(deltas(core, near[group], far[group], near_grads[group], far_grad, 896))
        other_delta[group] = to_core(own_delta[group])
        if group:
            out_sent = along(add(out_sent, out_part[group + 1]))
        else:
            layer_out = add(out_sent, out_part[0])
        parts = in_parts(core, own_delta[group], after(other_delta[group]), gate_proj, up_proj, chunk, 256)
        note(parts[0])
        for k, part in zip(groups[group], parts):
            in_part[k] = part
        if group == 1:
            in_sent = along(in_part[1])
        elif group == 2:
            in_sent = along(add(in_sent, in_part[2]))
    parts = [own_delta[k] for k in range(3)], [other_delta[k] for k in range(3)]
    gate_grad, up_grad = weight_grads(core, [after(inputs[0]), *inputs[1:]], *parts, 256)
    in_sent = along((in_sent.astype(F32) + in_part[3].astype(F32)).astype(BF16))
    in_grad = (in_sent.astype(F32) + in_part[0].astype(F32)).astype(BF16)
    return (layer_out, in_grad, gate_grad, up_grad, down_grad)


def solution(mesh):
    placed = (
        P(("groups", "col"), "row"),
        P("row", "col"),
        P("row", "col"),
        P("col", "row"),
        P(("groups", "col"), "row"),
    )
    paired = mesh.shape["row"] == 4 and mesh.shape["col"] == 4
    return jax.shard_map(
        functools.partial(paired_body, mesh.shape["col"]) if paired else general_body,
        mesh=mesh,
        in_specs=placed,
        out_specs=(
            P(("groups", "col"), "row"),
            P(("groups", "col"), "row"),
            P(("groups", "row"), "col"),
            P(("groups", "row"), "col"),
            P(("groups", "col"), "row"),
        ),
        check_vma=False,
    )
```

```python
import functools

import jax
import jax.numpy as jnp
from jax import lax
from jax.experimental import pallas as pl
from jax.experimental.pallas import tpu as pltpu
from jax.sharding import PartitionSpec as P

F32 = jnp.float32
BF16 = jnp.bfloat16
VMEM_LIMIT = 2**26 - 2**16
IN_TILE = 256


def swiglu_parts(gate_act, up_act):
    logistic = jax.nn.sigmoid(gate_act)
    swish_act = gate_act * logistic
    hidden = (swish_act * up_act).astype(BF16)
    return (logistic, swish_act, hidden)


def make_deltas(hid_grad, gate_act, up_act, logistic, swish_act):
    gate_delta = (hid_grad * up_act * logistic * (1.0 + gate_act * (1.0 - logistic))).astype(BF16)
    up_delta = (hid_grad * swish_act).astype(BF16)
    return (gate_delta, up_delta)


def last_product(left, right):
    return lax.dot_general(left, right, (((1,), (1,)), ((), ())), preferred_element_type=F32)


def first_product(left, right):
    return lax.dot_general(left, right, (((0,), (0,)), ((), ())), preferred_element_type=F32)


def plain_product(left, right):
    return lax.dot_general(left, right, (((1,), (0,)), ((), ())), preferred_element_type=F32)


def general_body(hidden_in, gate_proj, up_proj, down_proj, out_grad):
    inputs_all = lax.all_gather(hidden_in, "col", axis=0, tiled=True)
    gate_act, up_act = (
        lax.psum_scatter(
            plain_product(inputs_all, proj).astype(BF16), "row", scatter_dimension=0, tiled=True
        ).astype(F32)
        for proj in (gate_proj, up_proj)
    )
    logistic, swish_act, hidden = swiglu_parts(gate_act, up_act)
    hidden_all = lax.all_gather(hidden, "row", axis=0, tiled=True)
    layer_out = lax.psum_scatter(
        plain_product(hidden_all, down_proj).astype(BF16), "col", scatter_dimension=0, tiled=True
    )
    grads_all = lax.all_gather(out_grad, "col", axis=0, tiled=True)
    hid_grad = lax.psum_scatter(
        last_product(grads_all, down_proj).astype(BF16), "row", scatter_dimension=0, tiled=True
    ).astype(F32)
    gate_delta, up_delta = make_deltas(hid_grad, gate_act, up_act, logistic, swish_act)
    gate_full = lax.all_gather(gate_delta, "row", axis=0, tiled=True)
    up_full = lax.all_gather(up_delta, "row", axis=0, tiled=True)
    down_grad = first_product(hidden_all, grads_all).astype(BF16)
    gate_grad = first_product(inputs_all, gate_full).astype(BF16)
    up_grad = first_product(inputs_all, up_full).astype(BF16)
    in_grad = lax.psum_scatter(
        (last_product(gate_full, gate_proj) + last_product(up_full, up_proj)).astype(BF16),
        "col",
        scatter_dimension=0,
        tiled=True,
    )
    return (layer_out, in_grad, gate_grad, up_grad, down_grad)


def call(kernel, core, operands, in_specs, out_specs, out_shape, grid, scratch, flops, moved):
    return pl.pallas_call(
        kernel,
        grid_spec=pltpu.PrefetchScalarGridSpec(
            num_scalar_prefetch=1,
            grid=grid,
            in_specs=in_specs,
            out_specs=out_specs,
            scratch_shapes=scratch,
        ),
        out_shape=out_shape,
        compiler_params=pltpu.CompilerParams(vmem_limit_bytes=VMEM_LIMIT),
        cost_estimate=pl.CostEstimate(flops=1, bytes_accessed=1, transcendentals=0),
    )(core, *operands)


def whole(array):
    return pl.BlockSpec(array.shape, lambda i, core: (0,) * array.ndim, pipeline_mode=pl.Buffered(1))


def rows_of(refs, store):
    at = 0
    for ref in refs:
        store[at : at + ref.shape[0], :] = ref[...]
        at += ref.shape[0]


def project(half, inputs, weights, transposed, tile, groups, added=None):
    tokens = sum(array.shape[0] for array in inputs)
    depth = inputs[0].shape[1]
    units = weights[0].shape[0 if transposed else 1] // 2
    steps = units // tile
    count = len(weights)
    starts = [sum(groups[:index]) for index in range(len(groups))]

    def kernel(half_ref, *refs):
        step = pl.program_id(0)
        input_refs, refs = refs[: len(inputs)], refs[len(inputs) :]
        weight_refs, refs = refs[:count], refs[count:]
        if added is not None:
            added_refs, refs = refs[: len(added)], refs[len(added) :]
        out_refs = refs[: len(groups) * (1 if added is not None else count)]
        if len(inputs) > 1:
            left_ref = refs[len(out_refs)]

            @pl.when(step == 0)
            def _():
                rows_of(input_refs, left_ref)
        else:
            left_ref = input_refs[0]
        for index in range(count):

            @pl.when(step // steps == index)
            def _():
                product = last_product if transposed else plain_product
                total = product(left_ref[...], weight_refs[index][...])
                for group, (start, size) in enumerate(zip(starts, groups)):
                    part = total[start : start + size]
                    if added is not None:
                        part = part + added_refs[index * len(groups) + group][...].astype(F32)
                        out_refs[group][0] = part.astype(BF16)
                    else:
                        out_refs[index * len(groups) + group][...] = part.astype(BF16)

    def tile_at(i, index):
        return jnp.clip(i - index * steps, 0, steps - 1)

    def weight_spec(index):
        if transposed:
            return pl.BlockSpec((tile, depth), lambda i, half: (half[0] * steps + tile_at(i, index), 0))
        return pl.BlockSpec((depth, tile), lambda i, half: (0, half[0] * steps + tile_at(i, index)))

    single_specs = [
        pl.BlockSpec((size, tile), lambda i, half, index=index: (0, tile_at(i, index)))
        for index in range(count)
        for size in groups
    ]
    in_specs = [*map(whole, inputs), *map(weight_spec, range(count))]
    if added is None:
        out_specs = single_specs
        out_shape = [jax.ShapeDtypeStruct((size, units), BF16) for _ in range(count) for size in groups]
    else:
        in_specs += single_specs
        out_specs = [pl.BlockSpec((1, size, tile), lambda i, half: (i // steps, 0, i % steps)) for size in groups]
        out_shape = [jax.ShapeDtypeStruct((count, size, units), BF16) for size in groups]
    return call(
        kernel,
        half,
        [*inputs, *weights, *(added or ())],
        in_specs,
        out_specs,
        out_shape,
        (count * steps,),
        [pltpu.VMEM((tokens, depth), BF16)] if len(inputs) > 1 else [],
        2 * tokens * depth * units * count,
        2 * (count * units * (depth + tokens) + tokens * depth),
    )


def sums(near_ref, far_ref, index):
    return near_ref[index].astype(F32) + far_ref[index].astype(F32)


def activate(core, near, far, tile):
    _, tokens, units = near.shape

    def kernel(core_ref, near_ref, far_ref, out_ref):
        gate, up = sums(near_ref, far_ref, 0), sums(near_ref, far_ref, 1)
        out_ref[...] = (gate * jax.nn.sigmoid(gate) * up).astype(BF16)

    pair = pl.BlockSpec((2, tokens, tile), lambda i, core: (0, 0, i))
    return call(
        kernel,
        core,
        [near, far],
        [pair, pair],
        pl.BlockSpec((tokens, tile), lambda i, core: (0, i)),
        jax.ShapeDtypeStruct((tokens, units), BF16),
        (units // tile,),
        [],
        10 * tokens * units,
        10 * tokens * units,
    )


def deltas(core, near, far, near_grad, far_grad, row, tile):
    _, tokens, units = near.shape
    at = row // tokens

    def kernel(core_ref, near_ref, far_ref, near_grad_ref, far_grad_ref, out_ref):
        gate, up = sums(near_ref, far_ref, 0), sums(near_ref, far_ref, 1)
        grad = sums(near_grad_ref, far_grad_ref, 0)
        logistic = jax.nn.sigmoid(gate)
        out_ref[0] = (grad * up * logistic * (1.0 + gate * (1.0 - logistic))).astype(BF16)
        out_ref[1] = (grad * (gate * logistic)).astype(BF16)

    pair = pl.BlockSpec((2, tokens, tile), lambda i, core: (0, 0, i))
    single = pl.BlockSpec((1, tokens, tile), lambda i, core: (0, at, i))
    return call(
        kernel,
        core,
        [near, far, near_grad, far_grad],
        [pair, pair, single, single],
        pair,
        jax.ShapeDtypeStruct((2, tokens, units), BF16),
        (units // tile,),
        [],
        10 * tokens * units,
        16 * tokens * units,
    )


ANYWHERE = pl.BlockSpec(memory_space=pl.ANY)


class Loads:
    def __init__(self, semaphores):
        self.semaphores = semaphores
        self.copies = []

    def rows(self, refs, target, at=None):
        row, places = 0, []
        for ref in refs:
            size, width = ref.shape
            columns = slice(None) if at is None else pl.ds(at, width)
            places.append(len(self.copies))
            self.copies.append(
                pltpu.make_async_copy(
                    ref, target.at[pl.ds(row, size), columns], self.semaphores.at[len(self.copies)]
                )
            )
            row += size
        return places

    def start(self, places):
        for place in places:
            self.copies[place].start()

    def wait(self, places):
        for place in places:
            self.copies[place].wait()


def halves(core_ref, units):
    own = pl.multiple_of(core_ref[0] * units, 128)
    return own, pl.multiple_of(units - own, 128)


def out_parts(core, own, other, down_proj, chunk, tile):
    units, width = own[0].shape[1], down_proj.shape[1]
    tokens = sum(array.shape[0] for array in own)
    chunks = tokens // chunk

    def kernel(core_ref, *refs):
        own_refs, refs = refs[: len(own)], refs[len(own) :]
        other_refs, refs = refs[: len(other)], refs[len(other) :]
        own_down, other_down = refs[:2]
        out_refs = refs[2 : 2 + chunks]
        own_store, other_store = refs[2 + chunks :]

        @pl.when(pl.program_id(0) == 0)
        def _():
            rows_of(own_refs, own_store)
            rows_of(other_refs, other_store)

        total = plain_product(own_store[...], own_down[...])
        total = total + plain_product(other_store[...], other_down[...])
        for index, out_ref in enumerate(out_refs):
            out_ref[...] = total[index * chunk : (index + 1) * chunk].astype(BF16)

    return call(
        kernel,
        core,
        [*own, *other, down_proj, down_proj],
        [
            *map(whole, own),
            *map(whole, other),
            pl.BlockSpec((units, tile), lambda i, core: (core[0], i)),
            pl.BlockSpec((units, tile), lambda i, core: (1 - core[0], i)),
        ],
        [pl.BlockSpec((chunk, tile), lambda i, core: (0, i))] * chunks,
        [jax.ShapeDtypeStruct((chunk, width), BF16)] * chunks,
        (width // tile,),
        [pltpu.VMEM((tokens, units), BF16)] * 2,
        4 * tokens * units * width,
        2 * (2 * units * (width + tokens) + tokens * width),
    )


def in_parts(core, own, other, gate_proj, up_proj, chunk, tile):
    units, width, count = own[0].shape[2], gate_proj.shape[0], len(own)
    tokens = sum(array.shape[1] for array in own)
    chunks = tokens // chunk

    def kernel(core_ref, *refs):
        own_refs, other_refs, refs = refs[:count], refs[count : 2 * count], refs[2 * count :]
        gate_ref, up_ref = refs[:2]
        out_refs, (gate_left, up_left, semaphores) = refs[2 : 2 + chunks], refs[2 + chunks :]
        loads = Loads(semaphores)
        own_at, other_at = halves(core_ref, units)
        places = []
        for index, left in enumerate((gate_left, up_left)):
            places += loads.rows([ref.at[index] for ref in own_refs], left, own_at)
            places += loads.rows([ref.at[index] for ref in other_refs], left, other_at)

        @pl.when(pl.program_id(0) == 0)
        def _():
            loads.start(places)
            loads.wait(places)

        total = last_product(gate_left[...], gate_ref[...]) + last_product(up_left[...], up_ref[...])
        for index, out_ref in enumerate(out_refs):
            out_ref[...] = total[index * chunk : (index + 1) * chunk].astype(BF16)

    weight_spec = pl.BlockSpec((tile, 2 * units), lambda i, core: (i, 0))
    return call(
        kernel,
        core,
        [*own, *other, gate_proj, up_proj],
        [*[ANYWHERE] * (2 * count), weight_spec, weight_spec],
        [pl.BlockSpec((chunk, tile), lambda i, core: (0, i))] * chunks,
        [jax.ShapeDtypeStruct((chunk, width), BF16)] * chunks,
        (width // tile,),
        [*[pltpu.VMEM((tokens, 2 * units), BF16)] * 2, pltpu.SemaphoreType.DMA((4 * count,))],
        8 * tokens * units * width,
        2 * (4 * units * (width + tokens) + tokens * width),
    )


def down_weight_grad(core, own, other, grads, tile):
    units, width = own[0].shape[1], grads[0].shape[1]
    tokens = sum(array.shape[0] for array in grads)
    steps = units // tile

    def kernel(core_ref, *refs):
        own_refs, refs = refs[: len(own)], refs[len(own) :]
        other_refs, refs = refs[: len(other)], refs[len(other) :]
        grad_refs, refs = refs[: len(grads)], refs[len(grads) :]
        out_ref, left, right = refs
        step = pl.program_id(0)

        @pl.when(step == 0)
        def _():
            rows_of(own_refs, left.at[0])
            rows_of(other_refs, left.at[1])
            rows_of(grad_refs, right)

        at = pl.multiple_of((step % steps) * tile, 128)
        out_ref[...] = first_product(left[step // steps, :, pl.ds(at, tile)], right[...]).astype(BF16)

    def out_at(i, core):
        return (jnp.where(i < steps, core[0], 1 - core[0]) * steps + i % steps, 0)

    return call(
        kernel,
        core,
        [*own, *other, *grads],
        [*map(whole, own), *map(whole, other), *map(whole, grads)],
        pl.BlockSpec((tile, width), out_at),
        jax.ShapeDtypeStruct((2 * units, width), BF16),
        (2 * steps,),
        [pltpu.VMEM((2, tokens, units), BF16), pltpu.VMEM((tokens, width), BF16)],
        4 * tokens * units * width,
        2 * (2 * units * (width + tokens) + tokens * width),
    )


def weight_grads(core, inputs, own, other, tile):
    depth, units = inputs[0].shape[1], own[0].shape[2]
    tokens = sum(array.shape[0] for array in inputs)
    steps, count = depth // tile, len(own)

    def kernel(core_ref, *refs):
        input_refs, refs = refs[: len(inputs)], refs[len(inputs) :]
        own_refs, other_refs, refs = refs[:count], refs[count : 2 * count], refs[2 * count :]
        gate_ref, up_ref, left, gate_right, up_right, semaphores = refs
        step = pl.program_id(0)
        loads = Loads(semaphores)
        own_at, other_at = halves(core_ref, units)
        first, second = (
            loads.rows([ref.at[index] for ref in own_refs], right, own_at)
            + loads.rows([ref.at[index] for ref in other_refs], right, other_at)
            for index, right in enumerate((gate_right, up_right))
        )
        first = loads.rows(input_refs, left) + first

        @pl.when(step == 0)
        def _():
            loads.start(first)
            loads.start(second)
            loads.wait(first)

        @pl.when(step == steps)
        def _():
            loads.wait(second)

        columns = left[:, pl.ds(pl.multiple_of((step % steps) * tile, 128), tile)]

        @pl.when(step < steps)
        def _():
            gate_ref[...] = first_product(columns, gate_right[...]).astype(BF16)

        @pl.when(step >= steps)
        def _():
            up_ref[...] = first_product(columns, up_right[...]).astype(BF16)

    return call(
        kernel,
        core,
        [*inputs, *own, *other],
        [ANYWHERE] * (len(inputs) + 2 * count),
        [
            pl.BlockSpec((tile, 2 * units), lambda i, core: (jnp.clip(i, 0, steps - 1), 0)),
            pl.BlockSpec((tile, 2 * units), lambda i, core: (jnp.clip(i - steps, 0, steps - 1), 0)),
        ],
        [jax.ShapeDtypeStruct((depth, 2 * units), BF16)] * 2,
        (2 * steps,),
        [
            pltpu.VMEM((tokens, depth), BF16),
            *[pltpu.VMEM((tokens, 2 * units), BF16)] * 2,
            pltpu.SemaphoreType.DMA((len(inputs) + 4 * count,)),
        ],
        8 * tokens * units * depth,
        2 * (4 * units * (depth + tokens) + tokens * depth),
    )


def paired_body(cols, hidden_in, gate_proj, up_proj, down_proj, out_grad):
    chunk = hidden_in.shape[0]
    core = (lax.axis_index("row") % 2).astype(jnp.int32).reshape(1)
    other_core = 1 - core
    ring = [(i, (i + 1) % cols) for i in range(cols)]

    def along(array):
        return lax.ppermute(array, "col", ring)

    def back_along(array, places):
        return lax.ppermute(array, "col", [(i, (i - places) % cols) for i in range(cols)])

    def to_core(array):
        return lax.ppermute(array, "row", [(0, 1), (1, 0), (2, 3), (3, 2)])

    def to_chip(array):
        return lax.ppermute(array, "row", [(0, 2), (2, 0), (1, 3), (3, 1)])

    last = [None]

    def after(array, *others):
        others = [*others, *(last if last[0] is not None else ())]
        return lax.optimization_barrier((array, *others))[0] if others else array

    def note(array):
        last[0] = array
        return array

    inputs = [hidden_in]
    for _ in range(cols - 1):
        inputs.append(along(inputs[-1]))
    grads = [lax.optimization_barrier((out_grad, inputs[-1]))[0]]
    for _ in range(cols - 1):
        grads.append(along(grads[-1]))

    groups = [(0,), (1,), (2, 3)]
    near, far, own, other = [None] * 3, [None] * 3, [None] * 3, [None] * 3

    def act(group):
        own[group] = note(activate(core, near[group], after(far[group]), 896))
        other[group] = to_core(own[group])

    for index, group in enumerate(groups):
        chunks = [inputs[k] for k in group]
        sizes = [chunk * len(group)]
        first = after(chunks[-1])
        sent = project(other_core, [*chunks[:-1], first], [gate_proj, up_proj], False, 896, sizes)
        note(sent[0])
        (near[index],) = project(
            core, chunks, [gate_proj, up_proj], False, 896, sizes, list(map(to_core, sent))
        )
        note(near[index])
        far[index] = to_chip(near[index])
        if index:
            act(index - 1)

    sizes = [chunk, 3 * chunk]
    rows = [grads[k] for k in (1, 2, 3, 0)]
    sent = project(other_core, [*rows[:-1], after(rows[-1])], [down_proj], True, 896, sizes)
    note(sent[0])
    sent = project(core, rows, [down_proj], True, 896, sizes, list(map(to_core, sent)))
    note(sent[0])
    near_grads = {1: sent[0], 2: sent[1], 0: sent[1]}
    far_grads = {1: to_chip(sent[0]), 2: to_chip(sent[1])}
    far_grads[0] = far_grads[2]
    act(2)

    out_part = out_parts(core, own, [*other[:-1], after(other[-1])], down_proj, chunk, 512)
    note(out_part[0])
    out_came = {2: back_along(out_part[2], 2)}
    down_grad = note(down_weight_grad(core, own, [*other[:-1], after(other[-1])], grads, 896))

    own_delta, other_delta, in_came = {}, {}, {}

    def delta(group, *others):
        far_grad = after(far_grads[group], *others)
        row = 0 if group else 2 * chunk
        own_delta[group] = note(deltas(core, near[group], far[group], near_grads[group], far_grad, row, 896))
        other_delta[group] = to_core(own_delta[group])

    delta(1)
    out_came[1] = back_along(after(out_part[1]), 1)
    (part,) = in_parts(core, [own_delta[1]], [after(other_delta[1])], gate_proj, up_proj, chunk, IN_TILE)
    in_came[1] = back_along(note(part), 1)
    out_came[3] = back_along(after(out_part[3]), 3)
    delta(2, out_came[2])
    delta(0)
    parts = [own_delta[2], own_delta[0]], [other_delta[2], after(other_delta[0])]
    second, third, kept = in_parts(core, *parts, gate_proj, up_proj, chunk, IN_TILE)
    note(second)
    in_came[2], in_came[3] = back_along(second, 2), back_along(third, 3)
    parts = [own_delta[k] for k in range(3)], [other_delta[k] for k in range(3)]
    first = after(inputs[0], in_came[1], out_came[1], out_came[3])
    gate_grad, up_grad = weight_grads(core, [first, *inputs[1:]], *parts, 256)
    note(gate_grad)

    def total(first, came):
        parts = [after(first), *[came[k] for k in range(1, cols)]]
        return sum(part.astype(F32) for part in parts).astype(BF16)

    return (total(out_part[0], out_came), total(kept, in_came), gate_grad, up_grad, down_grad)


def solution(mesh):
    placed = (
        P(("groups", "col"), "row"),
        P("row", "col"),
        P("row", "col"),
        P("col", "row"),
        P(("groups", "col"), "row"),
    )
    paired = mesh.shape["row"] == 4 and mesh.shape["col"] == 4
    return jax.shard_map(
        functools.partial(paired_body, mesh.shape["col"]) if paired else general_body,
        mesh=mesh,
        in_specs=placed,
        out_specs=(
            P(("groups", "col"), "row"),
            P(("groups", "col"), "row"),
            P(("groups", "row"), "col"),
            P(("groups", "row"), "col"),
            P(("groups", "col"), "row"),
        ),
        check_vma=False,
    )
```

```python
import functools

import jax
import jax.numpy as jnp
from jax import lax
from jax.experimental import pallas as pl
from jax.experimental.pallas import tpu as pltpu
from jax.sharding import PartitionSpec as P

F32 = jnp.float32
BF16 = jnp.bfloat16
VMEM_LIMIT = 2**26 - 2**16
IN_TILE = 256


def swiglu_parts(gate_act, up_act):
    logistic = jax.nn.sigmoid(gate_act)
    swish_act = gate_act * logistic
    hidden = (swish_act * up_act).astype(BF16)
    return (logistic, swish_act, hidden)


def make_deltas(hid_grad, gate_act, up_act, logistic, swish_act):
    gate_delta = (hid_grad * up_act * logistic * (1.0 + gate_act * (1.0 - logistic))).astype(BF16)
    up_delta = (hid_grad * swish_act).astype(BF16)
    return (gate_delta, up_delta)


def last_product(left, right):
    return lax.dot_general(left, right, (((1,), (1,)), ((), ())), preferred_element_type=F32)


def first_product(left, right):
    return lax.dot_general(left, right, (((0,), (0,)), ((), ())), preferred_element_type=F32)


def plain_product(left, right):
    return lax.dot_general(left, right, (((1,), (0,)), ((), ())), preferred_element_type=F32)


def general_body(hidden_in, gate_proj, up_proj, down_proj, out_grad):
    inputs_all = lax.all_gather(hidden_in, "col", axis=0, tiled=True)
    gate_act, up_act = (
        lax.psum_scatter(
            plain_product(inputs_all, proj).astype(BF16), "row", scatter_dimension=0, tiled=True
        ).astype(F32)
        for proj in (gate_proj, up_proj)
    )
    logistic, swish_act, hidden = swiglu_parts(gate_act, up_act)
    hidden_all = lax.all_gather(hidden, "row", axis=0, tiled=True)
    layer_out = lax.psum_scatter(
        plain_product(hidden_all, down_proj).astype(BF16), "col", scatter_dimension=0, tiled=True
    )
    grads_all = lax.all_gather(out_grad, "col", axis=0, tiled=True)
    hid_grad = lax.psum_scatter(
        last_product(grads_all, down_proj).astype(BF16), "row", scatter_dimension=0, tiled=True
    ).astype(F32)
    gate_delta, up_delta = make_deltas(hid_grad, gate_act, up_act, logistic, swish_act)
    gate_full = lax.all_gather(gate_delta, "row", axis=0, tiled=True)
    up_full = lax.all_gather(up_delta, "row", axis=0, tiled=True)
    down_grad = first_product(hidden_all, grads_all).astype(BF16)
    gate_grad = first_product(inputs_all, gate_full).astype(BF16)
    up_grad = first_product(inputs_all, up_full).astype(BF16)
    in_grad = lax.psum_scatter(
        (last_product(gate_full, gate_proj) + last_product(up_full, up_proj)).astype(BF16),
        "col",
        scatter_dimension=0,
        tiled=True,
    )
    return (layer_out, in_grad, gate_grad, up_grad, down_grad)


def call(kernel, core, operands, in_specs, out_specs, out_shape, grid, scratch, flops, moved):
    return pl.pallas_call(
        kernel,
        grid_spec=pltpu.PrefetchScalarGridSpec(
            num_scalar_prefetch=1,
            grid=grid,
            in_specs=in_specs,
            out_specs=out_specs,
            scratch_shapes=scratch,
        ),
        out_shape=out_shape,
        compiler_params=pltpu.CompilerParams(vmem_limit_bytes=VMEM_LIMIT),
        cost_estimate=pl.CostEstimate(flops=1, bytes_accessed=1, transcendentals=0),
    )(core, *operands)


def whole(array):
    return pl.BlockSpec(array.shape, lambda i, core: (0,) * array.ndim, pipeline_mode=pl.Buffered(1))


def rows_of(refs, store):
    at = 0
    for ref in refs:
        store[at : at + ref.shape[0], :] = ref[...]
        at += ref.shape[0]


def project(half, inputs, weights, transposed, tile, groups, added=None):
    tokens = sum(array.shape[0] for array in inputs)
    depth = inputs[0].shape[1]
    units = weights[0].shape[0 if transposed else 1] // 2
    steps = units // tile
    count = len(weights)
    starts = [sum(groups[:index]) for index in range(len(groups))]

    def kernel(half_ref, *refs):
        step = pl.program_id(0)
        input_refs, refs = refs[: len(inputs)], refs[len(inputs) :]
        weight_refs, refs = refs[:count], refs[count:]
        if added is not None:
            added_refs, refs = refs[: len(added)], refs[len(added) :]
        out_refs = refs[: len(groups) * (1 if added is not None else count)]
        if len(inputs) > 1:
            left_ref = refs[len(out_refs)]

            @pl.when(step == 0)
            def _():
                rows_of(input_refs, left_ref)
        else:
            left_ref = input_refs[0]
        for index in range(count):

            @pl.when(step // steps == index)
            def _():
                product = last_product if transposed else plain_product
                total = product(left_ref[...], weight_refs[index][...])
                for group, (start, size) in enumerate(zip(starts, groups)):
                    part = total[start : start + size]
                    if added is not None:
                        part = part + added_refs[index * len(groups) + group][...].astype(F32)
                        out_refs[group][0] = part.astype(BF16)
                    else:
                        out_refs[index * len(groups) + group][...] = part.astype(BF16)

    def tile_at(i, index):
        return jnp.clip(i - index * steps, 0, steps - 1)

    def weight_spec(index):
        if transposed:
            return pl.BlockSpec((tile, depth), lambda i, half: (half[0] * steps + tile_at(i, index), 0))
        return pl.BlockSpec((depth, tile), lambda i, half: (0, half[0] * steps + tile_at(i, index)))

    single_specs = [
        pl.BlockSpec((size, tile), lambda i, half, index=index: (0, tile_at(i, index)))
        for index in range(count)
        for size in groups
    ]
    in_specs = [*map(whole, inputs), *map(weight_spec, range(count))]
    if added is None:
        out_specs = single_specs
        out_shape = [jax.ShapeDtypeStruct((size, units), BF16) for _ in range(count) for size in groups]
    else:
        in_specs += single_specs
        out_specs = [pl.BlockSpec((1, size, tile), lambda i, half: (i // steps, 0, i % steps)) for size in groups]
        out_shape = [jax.ShapeDtypeStruct((count, size, units), BF16) for size in groups]
    return call(
        kernel,
        half,
        [*inputs, *weights, *(added or ())],
        in_specs,
        out_specs,
        out_shape,
        (count * steps,),
        [pltpu.VMEM((tokens, depth), BF16)] if len(inputs) > 1 else [],
        2 * tokens * depth * units * count,
        2 * (count * units * (depth + tokens) + tokens * depth),
    )


def sums(near_ref, far_ref, index):
    return near_ref[index].astype(F32) + far_ref[index].astype(F32)


def activate(core, near, far, tile):
    _, tokens, units = near.shape

    def kernel(core_ref, near_ref, far_ref, out_ref):
        gate, up = sums(near_ref, far_ref, 0), sums(near_ref, far_ref, 1)
        out_ref[...] = (gate * jax.nn.sigmoid(gate) * up).astype(BF16)

    pair = pl.BlockSpec((2, tokens, tile), lambda i, core: (0, 0, i))
    return call(
        kernel,
        core,
        [near, far],
        [pair, pair],
        pl.BlockSpec((tokens, tile), lambda i, core: (0, i)),
        jax.ShapeDtypeStruct((tokens, units), BF16),
        (units // tile,),
        [],
        10 * tokens * units,
        10 * tokens * units,
    )


def deltas(core, near, far, near_grad, far_grad, row, tile):
    _, tokens, units = near.shape
    at = row // tokens

    def kernel(core_ref, near_ref, far_ref, near_grad_ref, far_grad_ref, out_ref):
        gate, up = sums(near_ref, far_ref, 0), sums(near_ref, far_ref, 1)
        grad = sums(near_grad_ref, far_grad_ref, 0)
        logistic = jax.nn.sigmoid(gate)
        out_ref[0] = (grad * up * logistic * (1.0 + gate * (1.0 - logistic))).astype(BF16)
        out_ref[1] = (grad * (gate * logistic)).astype(BF16)

    pair = pl.BlockSpec((2, tokens, tile), lambda i, core: (0, 0, i))
    single = pl.BlockSpec((1, tokens, tile), lambda i, core: (0, at, i))
    return call(
        kernel,
        core,
        [near, far, near_grad, far_grad],
        [pair, pair, single, single],
        pair,
        jax.ShapeDtypeStruct((2, tokens, units), BF16),
        (units // tile,),
        [],
        10 * tokens * units,
        16 * tokens * units,
    )


ANYWHERE = pl.BlockSpec(memory_space=pl.ANY)


class Loads:
    def __init__(self, semaphores):
        self.semaphores = semaphores
        self.copies = []

    def rows(self, refs, target, at=None):
        row, places = 0, []
        for ref in refs:
            size, width = ref.shape
            columns = slice(None) if at is None else pl.ds(at, width)
            places.append(len(self.copies))
            self.copies.append(
                pltpu.make_async_copy(
                    ref, target.at[pl.ds(row, size), columns], self.semaphores.at[len(self.copies)]
                )
            )
            row += size
        return places

    def start(self, places):
        for place in places:
            self.copies[place].start()

    def wait(self, places):
        for place in places:
            self.copies[place].wait()


def halves(core_ref, units):
    own = pl.multiple_of(core_ref[0] * units, 128)
    return own, pl.multiple_of(units - own, 128)


def out_parts(core, own, other, down_proj, chunk, tile):
    units, width = own[0].shape[1], down_proj.shape[1]
    tokens = sum(array.shape[0] for array in own)
    chunks = tokens // chunk

    def kernel(core_ref, *refs):
        own_refs, refs = refs[: len(own)], refs[len(own) :]
        other_refs, refs = refs[: len(other)], refs[len(other) :]
        own_down, other_down = refs[:2]
        out_refs = refs[2 : 2 + chunks]
        own_store, other_store = refs[2 + chunks :]

        @pl.when(pl.program_id(0) == 0)
        def _():
            rows_of(own_refs, own_store)
            rows_of(other_refs, other_store)

        total = plain_product(own_store[...], own_down[...])
        total = total + plain_product(other_store[...], other_down[...])
        for index, out_ref in enumerate(out_refs):
            out_ref[...] = total[index * chunk : (index + 1) * chunk].astype(BF16)

    return call(
        kernel,
        core,
        [*own, *other, down_proj, down_proj],
        [
            *map(whole, own),
            *map(whole, other),
            pl.BlockSpec((units, tile), lambda i, core: (core[0], i)),
            pl.BlockSpec((units, tile), lambda i, core: (1 - core[0], i)),
        ],
        [pl.BlockSpec((chunk, tile), lambda i, core: (0, i))] * chunks,
        [jax.ShapeDtypeStruct((chunk, width), BF16)] * chunks,
        (width // tile,),
        [pltpu.VMEM((tokens, units), BF16)] * 2,
        4 * tokens * units * width,
        2 * (2 * units * (width + tokens) + tokens * width),
    )


def in_parts(core, own, other, gate_proj, up_proj, chunk, tile):
    units, width, count = own[0].shape[2], gate_proj.shape[0], len(own)
    tokens = sum(array.shape[1] for array in own)
    chunks = tokens // chunk

    def kernel(core_ref, *refs):
        own_refs, other_refs, refs = refs[:count], refs[count : 2 * count], refs[2 * count :]
        gate_ref, up_ref = refs[:2]
        out_refs, (gate_left, up_left, semaphores) = refs[2 : 2 + chunks], refs[2 + chunks :]
        loads = Loads(semaphores)
        own_at, other_at = halves(core_ref, units)
        places = []
        for index, left in enumerate((gate_left, up_left)):
            places += loads.rows([ref.at[index] for ref in own_refs], left, own_at)
            places += loads.rows([ref.at[index] for ref in other_refs], left, other_at)

        @pl.when(pl.program_id(0) == 0)
        def _():
            loads.start(places)
            loads.wait(places)

        total = last_product(gate_left[...], gate_ref[...]) + last_product(up_left[...], up_ref[...])
        for index, out_ref in enumerate(out_refs):
            out_ref[...] = total[index * chunk : (index + 1) * chunk].astype(BF16)

    weight_spec = pl.BlockSpec((tile, 2 * units), lambda i, core: (i, 0))
    return call(
        kernel,
        core,
        [*own, *other, gate_proj, up_proj],
        [*[ANYWHERE] * (2 * count), weight_spec, weight_spec],
        [pl.BlockSpec((chunk, tile), lambda i, core: (0, i))] * chunks,
        [jax.ShapeDtypeStruct((chunk, width), BF16)] * chunks,
        (width // tile,),
        [*[pltpu.VMEM((tokens, 2 * units), BF16)] * 2, pltpu.SemaphoreType.DMA((4 * count,))],
        8 * tokens * units * width,
        2 * (4 * units * (width + tokens) + tokens * width),
    )


def down_weight_grad(core, own, other, grads, tile):
    units, width = own[0].shape[1], grads[0].shape[1]
    tokens = sum(array.shape[0] for array in grads)
    steps = units // tile

    def kernel(core_ref, *refs):
        own_refs, refs = refs[: len(own)], refs[len(own) :]
        other_refs, refs = refs[: len(other)], refs[len(other) :]
        grad_refs, refs = refs[: len(grads)], refs[len(grads) :]
        out_ref, left, right = refs
        step = pl.program_id(0)

        @pl.when(step == 0)
        def _():
            rows_of(own_refs, left.at[0])
            rows_of(other_refs, left.at[1])
            rows_of(grad_refs, right)

        at = pl.multiple_of((step % steps) * tile, 128)
        out_ref[...] = first_product(left[step // steps, :, pl.ds(at, tile)], right[...]).astype(BF16)

    def out_at(i, core):
        return (jnp.where(i < steps, core[0], 1 - core[0]) * steps + i % steps, 0)

    return call(
        kernel,
        core,
        [*own, *other, *grads],
        [*map(whole, own), *map(whole, other), *map(whole, grads)],
        pl.BlockSpec((tile, width), out_at),
        jax.ShapeDtypeStruct((2 * units, width), BF16),
        (2 * steps,),
        [pltpu.VMEM((2, tokens, units), BF16), pltpu.VMEM((tokens, width), BF16)],
        4 * tokens * units * width,
        2 * (2 * units * (width + tokens) + tokens * width),
    )


def weight_grads(core, inputs, own, other, tile):
    depth, units = inputs[0].shape[1], own[0].shape[2]
    tokens = sum(array.shape[0] for array in inputs)
    steps, count = depth // tile, len(own)

    def kernel(core_ref, *refs):
        input_refs, refs = refs[: len(inputs)], refs[len(inputs) :]
        own_refs, other_refs, refs = refs[:count], refs[count : 2 * count], refs[2 * count :]
        gate_ref, up_ref, left, gate_right, up_right, semaphores = refs
        step = pl.program_id(0)
        loads = Loads(semaphores)
        own_at, other_at = halves(core_ref, units)
        first, second = (
            loads.rows([ref.at[index] for ref in own_refs], right, own_at)
            + loads.rows([ref.at[index] for ref in other_refs], right, other_at)
            for index, right in enumerate((gate_right, up_right))
        )
        first = loads.rows(input_refs, left) + first

        @pl.when(step == 0)
        def _():
            loads.start(first)
            loads.start(second)
            loads.wait(first)

        @pl.when(step == steps)
        def _():
            loads.wait(second)

        columns = left[:, pl.ds(pl.multiple_of((step % steps) * tile, 128), tile)]

        @pl.when(step < steps)
        def _():
            gate_ref[...] = first_product(columns, gate_right[...]).astype(BF16)

        @pl.when(step >= steps)
        def _():
            up_ref[...] = first_product(columns, up_right[...]).astype(BF16)

    return call(
        kernel,
        core,
        [*inputs, *own, *other],
        [ANYWHERE] * (len(inputs) + 2 * count),
        [
            pl.BlockSpec((tile, 2 * units), lambda i, core: (jnp.clip(i, 0, steps - 1), 0)),
            pl.BlockSpec((tile, 2 * units), lambda i, core: (jnp.clip(i - steps, 0, steps - 1), 0)),
        ],
        [jax.ShapeDtypeStruct((depth, 2 * units), BF16)] * 2,
        (2 * steps,),
        [
            pltpu.VMEM((tokens, depth), BF16),
            *[pltpu.VMEM((tokens, 2 * units), BF16)] * 2,
            pltpu.SemaphoreType.DMA((len(inputs) + 4 * count,)),
        ],
        8 * tokens * units * depth,
        2 * (4 * units * (depth + tokens) + tokens * depth),
    )


def paired_body(cols, hidden_in, gate_proj, up_proj, down_proj, out_grad):
    chunk = hidden_in.shape[0]
    core = (lax.axis_index("row") % 2).astype(jnp.int32).reshape(1)
    other_core = 1 - core
    ring = [(i, (i + 1) % cols) for i in range(cols)]

    def along(array):
        return lax.ppermute(array, "col", ring)

    def back_along(array, places):
        return lax.ppermute(array, "col", [(i, (i - places) % cols) for i in range(cols)])

    def to_core(array):
        return lax.ppermute(array, "row", [(0, 1), (1, 0), (2, 3), (3, 2)])

    def to_chip(array):
        return lax.ppermute(array, "row", [(0, 2), (2, 0), (1, 3), (3, 1)])

    last = [None]

    def after(array, *others):
        others = [*others, *(last if last[0] is not None else ())]
        return lax.optimization_barrier((array, *others))[0] if others else array

    def note(array):
        last[0] = array
        return array

    inputs = [hidden_in]
    for _ in range(cols - 1):
        inputs.append(along(inputs[-1]))
    grads = [lax.optimization_barrier((out_grad, inputs[-1]))[0]]
    for _ in range(cols - 1):
        grads.append(along(grads[-1]))

    groups = [(0,), (1,), (2, 3)]
    near, far, own, other = [None] * 3, [None] * 3, [None] * 3, [None] * 3

    def act(group):
        own[group] = note(activate(core, near[group], after(far[group]), 1792))
        other[group] = to_core(own[group])

    for index, group in enumerate(groups):
        chunks = [inputs[k] for k in group]
        sizes = [chunk * len(group)]
        first = after(chunks[-1])
        sent = project(other_core, [*chunks[:-1], first], [gate_proj, up_proj], False, 1792, sizes)
        note(sent[0])
        (near[index],) = project(
            core, chunks, [gate_proj, up_proj], False, 1792, sizes, list(map(to_core, sent))
        )
        note(near[index])
        far[index] = to_chip(near[index])
        if index:
            act(index - 1)

    sizes = [chunk, 3 * chunk]
    rows = [grads[k] for k in (1, 2, 3, 0)]
    sent = project(other_core, [*rows[:-1], after(rows[-1])], [down_proj], True, 1792, sizes)
    note(sent[0])
    sent = project(core, rows, [down_proj], True, 1792, sizes, list(map(to_core, sent)))
    note(sent[0])
    near_grads = {1: sent[0], 2: sent[1], 0: sent[1]}
    far_grads = {1: to_chip(sent[0]), 2: to_chip(sent[1])}
    far_grads[0] = far_grads[2]
    act(2)

    out_part = out_parts(core, own, [*other[:-1], after(other[-1])], down_proj, chunk, 512)
    note(out_part[0])
    out_came = {2: back_along(out_part[2], 2)}
    down_grad = note(down_weight_grad(core, own, [*other[:-1], after(other[-1])], grads, 896))

    own_delta, other_delta, in_came = {}, {}, {}

    def delta(group, *others):
        far_grad = after(far_grads[group], *others)
        row = 0 if group else 2 * chunk
        own_delta[group] = note(deltas(core, near[group], far[group], near_grads[group], far_grad, row, 1792))
        other_delta[group] = to_core(own_delta[group])

    delta(1)
    out_came[1] = back_along(after(out_part[1]), 1)
    (part,) = in_parts(core, [own_delta[1]], [after(other_delta[1])], gate_proj, up_proj, chunk, IN_TILE)
    in_came[1] = back_along(note(part), 1)
    out_came[3] = back_along(after(out_part[3]), 3)
    delta(2, out_came[2])
    delta(0)
    parts = [own_delta[2], own_delta[0]], [other_delta[2], after(other_delta[0])]
    second, third, kept = in_parts(core, *parts, gate_proj, up_proj, chunk, IN_TILE)
    note(second)
    in_came[2], in_came[3] = back_along(second, 2), back_along(third, 3)
    parts = [own_delta[k] for k in range(3)], [other_delta[k] for k in range(3)]
    first = after(inputs[0], in_came[1], out_came[1], out_came[3])
    gate_grad, up_grad = weight_grads(core, [first, *inputs[1:]], *parts, 256)
    note(gate_grad)

    def total(first, came):
        parts = [after(first), *[came[k] for k in range(1, cols)]]
        return sum(part.astype(F32) for part in parts).astype(BF16)

    return (total(out_part[0], out_came), total(kept, in_came), gate_grad, up_grad, down_grad)


def solution(mesh):
    placed = (
        P(("groups", "col"), "row"),
        P("row", "col"),
        P("row", "col"),
        P("col", "row"),
        P(("groups", "col"), "row"),
    )
    paired = mesh.shape["row"] == 4 and mesh.shape["col"] == 4
    return jax.shard_map(
        functools.partial(paired_body, mesh.shape["col"]) if paired else general_body,
        mesh=mesh,
        in_specs=placed,
        out_specs=(
            P(("groups", "col"), "row"),
            P(("groups", "col"), "row"),
            P(("groups", "row"), "col"),
            P(("groups", "row"), "col"),
            P(("groups", "col"), "row"),
        ),
        check_vma=False,
    )
```
